32 devices in a mesh: gx: 4 (over z), gy: 4 (over x, core), gz: 2 (over y).
Axes of the slice: x: 2, y: 2, z: 4, core: 2. Of those that a mesh axis runs over, the one named last changes fastest.
Arguments:
- density: float32 [3, 64, 256, 256], P(None, 'gx', 'gy', 'gz'), may hold values from -6 to 6
- efficiency: float32 [64, 256, 256], P('gx', 'gy', 'gz'), may hold values from 0.5 to 2
Outputs:
- ionized: float32 [3, 64, 256, 256], P(None, 'gx', 'gy', 'gz')
The draws below stay inside these ranges and needn't reach their ends.
All inputs are finite; a program needn't handle non-finite values.
Results may differ from the reference program's by a relative error of at most 0.00005.
Values sent between devices are 32-bit elements; how exact they have to be, the bound alone decides.
A program may use at most 128 MiB of HBM per device.

```python
import math
import jax
import jax.numpy as jnp

SNAPS = 3
R_SMALL = 4
R_LARGE = 8
NX = 64
NY = 256
NZ = 256


def levels(key, shape, cuts, smallest, top_value):
    gain = 1.0
    for axis_at, blocks in cuts:
        steps = jax.random.uniform(jax.random.fold_in(jax.random.fold_in(key, 6), axis_at), (blocks,), jnp.float32, smallest / len(cuts), top_value / len(cuts))
        gain = gain * jnp.repeat(jnp.exp(steps), shape[axis_at] // blocks).reshape((-1,) + (1,) * (len(shape) - 1 - axis_at))
    return gain


def gaussian(own_key, dims, width, bound, split=(), kind=jnp.bfloat16):
    factor_of = levels(own_key, dims, split, -0.22, 0.18) if split else 1.0
    values = jax.random.normal(own_key, dims, jnp.float32) * width * factor_of
    return jnp.minimum(jnp.maximum(values, -bound), bound).astype(kind)


def setup_inputs(seed: int = 0) -> dict:
    splits = jax.random.split(jax.random.key(seed), 3)
    return {
        "density": gaussian(splits[0], (SNAPS, NX, NY, NZ), 1.0, 6.0, ((1, 4), (2, 4), (3, 2)), jnp.float32),
        "efficiency": jnp.clip(jnp.exp(math.log(2.0) - 1.3862944 * jax.random.uniform(splits[1], (NX, NY, NZ), jnp.float32) ** levels(splits[1], (NX, NY, NZ), ((0, 4), (1, 4), (2, 2)), -0.2, 0.2)), 0.5, 2.0),
    }


def profile(radius):
    offsets = jnp.arange(-radius, radius + 1).astype(jnp.float32)
    raw_weights = 1.0 - (offsets / (radius + 1.0)) ** 2
    return raw_weights / jnp.sqrt(jnp.sum(raw_weights * raw_weights))

def smooth(volume, radius):
    weights = profile(radius)
    for axis_dim in (3, 2, 1):
        total = jnp.zeros_like(volume)
        for index in range(2 * radius + 1):
            total = total + weights[index] * jnp.roll(volume, radius - index, axis_dim)
        volume = total
    return volume

def reference(density, efficiency):
    smooth_small = smooth(density, R_SMALL)
    smooth_large = smooth(density, R_LARGE)
    level_small = efficiency[None] * smooth_small - 0.3
    level_large = efficiency[None] * smooth_large - 0.1
    return jnp.clip(0.5 + 0.25 * jnp.maximum(level_small, level_large), 0.0, 1.0)
```

```python
import math

import jax
import jax.numpy as jnp
from jax import lax
from jax.experimental import pallas as pl
from jax.experimental.pallas import tpu as pltpu
from jax.sharding import PartitionSpec as P

R_SMALL = 4
R_LARGE = 8
RADII = (R_SMALL, R_LARGE)
H = R_LARGE
GROUP = 16
STRIP = 32
LATE = 4
F32 = jnp.float32
BF16 = jnp.bfloat16
MESH = pl.DeviceIdType.MESH


def scale_of(radius):
    raw = [(radius + 1) ** 2 - k * k for k in range(-radius, radius + 1)]
    return 1.0 / math.sqrt(sum(value * value for value in raw)) ** 3


def band(offset, radius):
    value = (radius + 1) ** 2 - offset * offset
    return jnp.where(jnp.abs(offset) <= radius, value, 0).astype(F32).astype(BF16)


def split(value):
    high = value.astype(BF16)
    return high, (value - high.astype(F32)).astype(BF16)


def iota(shape, dim):
    return lax.broadcasted_iota(jnp.int32, shape, dim)


def kernel(dens, eff, outv, ext, effv, xb, zb, zm, zsend, zrecv, wy, wm, wh, wl, late, tsend, trecv,
           up_in, wrap_in, beside_in, peers_in, sent, e_recv, m_recv, l_recv, t_recv, y_recv, f_recv,
           z_recv, own_sem, eff_sem):
    snaps, nx, ny, nz = dens.shape
    rows = ny + 2 * H
    groups = rows // GROUP
    strips = ny // STRIP
    wide = STRIP + 2 * H
    inner = ny - 2 * H
    final = snaps - 1
    units = snaps * strips
    everything = pl.ds(0, snaps)
    near = {}
    for axis in ("gx", "gy", "gz"):
        count = lax.axis_size(axis)
        me = lax.axis_index(axis)
        near[axis] = (lax.rem(me + 1, count), lax.rem(me + count - 1, count))
    up, down = ({"gx": near["gx"][d]} for d in range(2))
    peers = [{axis: near[axis][d]} for axis in ("gy", "gz") for d in range(2)]
    first = lax.axis_index("gx") == 0
    last = lax.axis_index("gx") == lax.axis_size("gx") - 1

    own_copy = pltpu.make_async_copy(
        dens, ext.at[everything, pl.ds(H, nx), pl.ds(H, ny)], own_sem)
    eff_copy = pltpu.make_async_copy(eff, effv, eff_sem)

    def landed(ref, sem):
        pltpu.make_async_copy(ref, ref, sem).wait()

    def edge_copies(d):
        source = nx - H if d == 0 else 0
        target = 0 if d == 0 else nx + H
        return [pltpu.make_async_remote_copy(
            src_ref=dens.at[everything, pl.ds(source, H), pl.ds(start, H)],
            dst_ref=ext.at[everything, pl.ds(target, H), pl.ds(H + start, H)],
            send_sem=sent.at[0], recv_sem=e_recv,
            device_id=up if d == 0 else down, device_id_type=MESH) for start in (0, ny - H)]

    def middle_copy(s, d):
        count = H - LATE if s == final else H
        skip = H - count if d == 0 else 0
        source = (nx - H if d == 0 else 0) + skip
        target = (0 if d == 0 else nx + H) + skip
        return pltpu.make_async_remote_copy(
            src_ref=dens.at[s, pl.ds(source, count), pl.ds(H, inner)],
            dst_ref=ext.at[s, pl.ds(target, count), pl.ds(2 * H, inner)],
            send_sem=sent.at[0], recv_sem=m_recv.at[s],
            device_id=up if d == 0 else down, device_id_type=MESH)

    def late_copy(d):
        source = nx - H if d == 0 else H - LATE
        return pltpu.make_async_remote_copy(
            src_ref=dens.at[final, pl.ds(source, LATE), pl.ds(H, inner)],
            dst_ref=late.at[d],
            send_sem=sent.at[0], recv_sem=l_recv,
            device_id=up if d == 0 else down, device_id_type=MESH)

    def t_copy(d):
        return pltpu.make_async_remote_copy(
            src_ref=tsend.at[d], dst_ref=trecv.at[d],
            send_sem=sent.at[1], recv_sem=t_recv,
            device_id=up if d == 0 else down, device_id_type=MESH)

    def y_copy(d):
        source = ny - H if d == 0 else 0
        target = 0 if d == 0 else ny + H
        return pltpu.make_async_remote_copy(
            src_ref=dens.at[everything, pl.ds(0, nx), pl.ds(source, H)],
            dst_ref=ext.at[everything, pl.ds(H, nx), pl.ds(target, H)],
            send_sem=sent.at[2], recv_sem=y_recv,
            device_id={"gy": near["gy"][d]}, device_id_type=MESH)

    def f_copy(q, d):
        planes = 0 if q == 0 else nx + H
        source = ny if d == 0 else H
        target = 0 if d == 0 else ny + H
        return pltpu.make_async_remote_copy(
            src_ref=ext.at[everything, pl.ds(planes, H), pl.ds(source, H)],
            dst_ref=ext.at[everything, pl.ds(planes, H), pl.ds(target, H)],
            send_sem=sent.at[3], recv_sem=f_recv,
            device_id={"gy": near["gy"][d]}, device_id_type=MESH)

    def z_copy(u, d):
        return pltpu.make_async_remote_copy(
            src_ref=zsend.at[u, d], dst_ref=zrecv.at[u, d],
            send_sem=sent.at[4], recv_sem=z_recv.at[u],
            device_id={"gz": near["gz"][d]}, device_id_type=MESH)

    def tell(sem, device):
        pl.semaphore_signal(sem, inc=1, device_id=device, device_id_type=MESH)

    def start(*copies):
        for copy in copies:
            copy.start()

    own_copy.start()
    eff_copy.start()

    barrier = pltpu.get_barrier_semaphore()

    @pl.when(first)
    def _():
        tell(barrier, up)
        for peer in peers:
            tell(barrier, peer)
        pl.semaphore_wait(barrier, len(peers))

    @pl.when(jnp.logical_not(first))
    def _():
        pl.semaphore_wait(barrier, 1)

        @pl.when(jnp.logical_not(last))
        def _():
            tell(barrier, up)
        tell(up_in, down)

        @pl.when(last)
        def _():
            tell(wrap_in, up)
            for pair in zip(edge_copies(0), edge_copies(1)):
                start(*pair)
            start(middle_copy(0, 0), middle_copy(0, 1))

        @pl.when(jnp.logical_not(last))
        def _():
            start(*edge_copies(1), middle_copy(0, 1))

    @pl.when(jnp.logical_not(last))
    def _():
        pl.semaphore_wait(up_in, 1)
        start(*edge_copies(0))

        @pl.when(jnp.logical_not(first))
        def _():
            start(middle_copy(0, 0))

    own_copy.wait()
    slots = nz // (2 * H)
    parts = slots // LATE
    tall = inner // parts
    slot_of = lax.div(iota((tall, nz), 1), 2 * H)
    for d in range(2):
        packed = jnp.zeros((tall, nz), F32)
        for p in range(LATE):
            for g in range(parts):
                slot = p * parts + g
                block = ext[final, (nx if d == 0 else 2 * H - LATE) + p, pl.ds(2 * H + g * tall, tall)]
                rolled = pltpu.roll(block, (slot * 2 * H + H) % nz, 1)
                packed = jnp.where(slot_of == slot, rolled, packed)
        tsend[d] = packed

    def rest(d):
        return [t_copy(d)] + [middle_copy(s, d) for s in range(1, snaps)] + [late_copy(d)]

    def meet_peers():
        for peer in peers:
            tell(beside_in, peer)
        pl.semaphore_wait(beside_in, len(peers))
        tell(peers_in, up)

    @pl.when(first)
    def _():
        meet_peers()
        pl.semaphore_wait(wrap_in, 1)
        start(*edge_copies(1), middle_copy(0, 0), middle_copy(0, 1))
        for pair in zip(rest(0), rest(1)):
            start(*pair)

    @pl.when(jnp.logical_not(first))
    def _():
        for pair in zip(rest(0), rest(1)):
            start(*pair)

    for f, radius in enumerate(RADII):
        shape = (STRIP, wide)
        along = band(iota(shape, 1) - iota(shape, 0) - H, radius)
        wy[f] = jnp.concatenate([along, along], axis=1)
        shape = (nz, nz)
        along = band(iota(shape, 1) - iota(shape, 0), radius)
        wm[f] = jnp.concatenate([along, along], axis=0)
        shape = (nx * H, nz)
        slot = lax.div(iota(shape, 0), H)
        cell = lax.rem(iota(shape, 0), H)
        lane = iota(shape, 1)
        low = band(cell - H - lane, radius)
        high = band(cell + nz - lane, radius)
        zero = jnp.zeros_like(low)
        for p in range(nx):
            low_p = jnp.where(slot == p, low, zero)
            high_p = jnp.where(slot == (p + 1) % nx, high, zero)
            wh[f, p // 2, pl.ds(0, nx * H), pl.ds((p % 2) * nz, nz)] = low_p
            wh[f, p // 2, pl.ds(nx * H, nx * H), pl.ds((p % 2) * nz, nz)] = high_p
    shape = (ny, inner)
    along = band(iota(shape, 1) + H - iota(shape, 0), R_LARGE)
    wl[...] = jnp.concatenate([along, along], axis=1)

    @pl.when(jnp.logical_not(first))
    def _():
        pl.semaphore_wait(peers_in, 1)

        @pl.when(jnp.logical_not(last))
        def _():
            meet_peers()

    for d in range(2):
        y_copy(d).start()
    landed(ext.at[everything, pl.ds(0, 2 * H), pl.ds(0, 2 * H)], e_recv)
    for d in range(2):
        for q in range(2):
            f_copy(q, d).start()

    def smooth_x(field, start, g):
        base = g * GROUP

        def one(i, carry):
            def plane(k):
                return field[i + (H + k), pl.ds(start, GROUP)]

            center = plane(0)
            sums = [center * float((radius + 1) ** 2) for radius in RADII]
            for k in range(1, R_LARGE + 1):
                pair = plane(-k) + plane(k)
                for f, radius in enumerate(RADII):
                    if k <= radius:
                        sums[f] = sums[f] + pair * float((radius + 1) ** 2 - k * k)
            for f in range(2):
                high, low = split(sums[f])
                xb[f, i, pl.ds(base, GROUP)] = high
                xb[f, i, pl.ds(rows + base, GROUP)] = low
            return carry

        lax.fori_loop(0, nx, one, 0, unroll=16)

    lane_slots = lax.div(iota((STRIP, nz), 1), H)

    def smooth_y(u):
        base = (u % strips) * STRIP
        for f in range(2):
            to_up = jnp.zeros((STRIP, nz), F32)
            to_down = jnp.zeros((STRIP, nz), F32)
            for p in range(0, nx, 2):
                both = jnp.concatenate(
                    [jnp.concatenate([xb[f, p + j, pl.ds(base, wide)],
                                      xb[f, p + j, pl.ds(rows + base, wide)]], axis=0)
                     for j in range(2)], axis=1)
                done = jnp.dot(wy[f], both, preferred_element_type=F32)
                for j in range(2):
                    value = done[:, j * nz:(j + 1) * nz]
                    rolled = pltpu.roll(value, ((p + j + 1) * H) % nz, 1)
                    to_up = jnp.where(lane_slots == p + j, rolled, to_up)
                    to_down = jnp.where(lane_slots == (p + j + 1) % nx, rolled, to_down)
                    high, low = split(value)
                    zb[f, p + j, :, pl.ds(0, nz)] = high
                    zb[f, p + j, :, pl.ds(nz, nz)] = low
            zsend[u, 0, pl.ds(f * STRIP, STRIP)] = to_up
            zsend[u, 1, pl.ds(f * STRIP, STRIP)] = to_down
        for d in range(2):
            z_copy(u, d).start()

    def main_z(u):
        slot = u % 2
        for f in range(2):
            for p in range(0, nx, 8):
                block = zb[f, pl.ds(p, 8)].reshape(8 * STRIP, 2 * nz)
                done = jnp.dot(block, wm[f], preferred_element_type=F32)
                zm[slot, f, pl.ds(p, 8)] = done.reshape(8, STRIP, nz)

    def ionized(small, total, share):
        large = share * (total * scale_of(R_LARGE)) - 0.1
        return jnp.clip(0.5 + 0.25 * jnp.maximum(small, large), 0.0, 1.0)

    def finish(u):
        slot = u % 2
        s, h = divmod(u, strips)
        part = pl.ds(h * STRIP, STRIP)
        landed(zrecv.at[u], z_recv.at[u])
        halves = []
        for f in range(2):
            own = pl.ds(f * STRIP, STRIP)
            packed = jnp.concatenate([zrecv[u, 0, own], zrecv[u, 1, own]], axis=1)
            halves.append(jnp.concatenate(split(packed), axis=0))
        for p in range(0, nx, 2):
            open_still = s == final and (p < LATE or p >= nx - LATE)
            sums = []
            for f in range(2):
                done = jnp.dot(halves[f], wh[f, p // 2], preferred_element_type=F32)
                done = done[:STRIP] + done[STRIP:]
                sums.append([zm[slot, f, p + j] + done[:, j * nz:(j + 1) * nz] for j in range(2)])
            for j in range(2):
                small = effv[p + j, part] * (sums[0][j] * scale_of(R_SMALL)) - 0.3
                if open_still:
                    outv[s, p + j, part] = small
                    zm[slot, 1, p + j] = sums[1][j]
                else:
                    outv[s, p + j, part] = ionized(small, sums[1][j], effv[p + j, part])

    def unpack():
        landed(trecv, t_recv)
        lane = iota((tall, nz), 1)
        outer = (lane < H) | (lane >= nz - H)
        for d in range(2):
            packed = trecv[d]
            for p in range(LATE):
                for g in range(parts):
                    slot = p * parts + g
                    block = pltpu.roll(packed, (2 * nz - slot * 2 * H - H) % nz, 1)
                    ext[final, (0 if d == 0 else nx + 2 * H - LATE) + p,
                        pl.ds(2 * H + g * tall, tall)] = jnp.where(outer, block, 0.0)

    def add_late():
        landed(late, l_recv)
        lane = iota((inner, nz), 1)
        inside = (lane >= H) & (lane < nz - H)
        moved = []
        for d in range(2):
            planes = [jnp.where(inside, late[d, p], 0.0) for p in range(LATE)]
            for i in range(LATE):
                total = None
                for e in (range(i, LATE) if d == 0 else range(i + 1)):
                    k = H + i - e if d == 0 else H + e - i
                    term = planes[e] * float((R_LARGE + 1) ** 2 - k * k)
                    total = term if total is None else total + term
                moved.append(jnp.concatenate(split(total), axis=0))
        blocks = []
        for p in range(0, 2 * LATE, 2):
            both = jnp.concatenate(moved[p:p + 2], axis=1)
            done = jnp.dot(wl[...], both, preferred_element_type=F32)
            for j in range(2):
                blocks.append(jnp.concatenate(split(done[:, j * nz:(j + 1) * nz]), axis=1))
        for n, block in enumerate(blocks):
            p = n if n < LATE else nx - 2 * LATE + n
            done = jnp.dot(block, wm[1], preferred_element_type=F32)
            for h in range(strips):
                part = pl.ds(h * STRIP, STRIP)
                total = zm[(final * strips + h) % 2, 1, p] + done[h * STRIP:(h + 1) * STRIP]
                outv[final, p, part] = ionized(outv[final, p, part], total, effv[p, part])

    landed(ext.at[everything, pl.ds(0, nx), pl.ds(0, 2 * H)], y_recv)
    landed(ext.at[everything, pl.ds(0, 2 * H), pl.ds(0, 2 * H)], f_recv)
    eff_copy.wait()
    for s in range(snaps):
        for g in (0, groups - 1):
            smooth_x(ext.at[s], g * GROUP, g)
        if s == final:
            unpack()
        count = H - LATE if s == final else H
        landed(ext.at[s, pl.ds(0, 2 * count), pl.ds(0, inner)], m_recv.at[s])
        for g in range(1, groups - 1):
            smooth_x(ext.at[s], g * GROUP, g)
        for u in range(s * strips, (s + 1) * strips):
            smooth_y(u)
            main_z(u)
        for u in range(s * strips, (s + 1) * strips):
            finish(u)
    add_late()

    landed(ext.at[everything, pl.ds(0, 2 * H), pl.ds(0, ny)], sent.at[0])
    landed(tsend, sent.at[1])
    landed(ext.at[everything, pl.ds(0, nx), pl.ds(0, 2 * H)], sent.at[2])
    landed(ext.at[everything, pl.ds(0, 2 * H), pl.ds(0, 2 * H)], sent.at[3])
    landed(zsend, sent.at[4])


def on_device(density, efficiency):
    snaps, nx, ny, nz = density.shape
    rows = ny + 2 * H
    inner = ny - 2 * H
    tall = inner * LATE * 2 * H // nz
    units = snaps * (ny // STRIP)
    dma = pltpu.SemaphoreType.DMA
    told = pltpu.SemaphoreType.REGULAR
    return pl.pallas_call(
        kernel,
        out_shape=pltpu.VMEM(density.shape, F32),
        in_specs=[pl.BlockSpec(memory_space=pl.ANY)] * 2,
        out_specs=pl.BlockSpec(memory_space=pltpu.VMEM),
        scratch_shapes=[
            pltpu.VMEM((snaps, nx + 2 * H, rows, nz), F32),
            pltpu.VMEM((nx, ny, nz), F32),
            pltpu.VMEM((2, nx, 2 * rows, nz), BF16),
            pltpu.VMEM((2, nx, STRIP, 2 * nz), BF16),
            pltpu.VMEM((2, 2, nx, STRIP, nz), F32),
            pltpu.VMEM((units, 2, 2 * STRIP, nx * H), F32),
            pltpu.VMEM((units, 2, 2 * STRIP, nx * H), F32),
            pltpu.VMEM((2, STRIP, 2 * (STRIP + 2 * H)), BF16),
            pltpu.VMEM((2, 2 * nz, nz), BF16),
            pltpu.VMEM((2, nx // 2, 2 * nx * H, 2 * nz), BF16),
            pltpu.VMEM((ny, 2 * inner), BF16),
            pltpu.VMEM((2, LATE, inner, nz), F32),
            pltpu.VMEM((2, tall, nz), F32),
            pltpu.VMEM((2, tall, nz), F32),
            told, told, told, told,
            dma((5,)), dma, dma((snaps,)), dma, dma, dma, dma, dma((units,)), dma, dma,
        ],
        compiler_params=pltpu.CompilerParams(
            collective_id=0, has_side_effects=True),
    )(density, efficiency)


def solution(mesh):
    placed = (P(None, "gx", "gy", "gz"), P("gx", "gy", "gz"))
    return jax.shard_map(
        on_device, mesh=mesh, in_specs=placed, out_specs=P(None, "gx", "gy", "gz"), check_vma=False
    )
```

```python
import math

import jax
import jax.numpy as jnp
from jax import lax
from jax.experimental import pallas as pl
from jax.experimental.pallas import tpu as pltpu
from jax.sharding import PartitionSpec as P

R_SMALL = 4
R_LARGE = 8
RADII = (R_SMALL, R_LARGE)
H = R_LARGE
GROUP = 16
STRIP = 32
LATE = 4
F32 = jnp.float32
BF16 = jnp.bfloat16
MESH = pl.DeviceIdType.MESH


def scale_of(radius):
    raw = [(radius + 1) ** 2 - k * k for k in range(-radius, radius + 1)]
    return 1.0 / math.sqrt(sum(value * value for value in raw)) ** 3


def band(offset, radius):
    value = (radius + 1) ** 2 - offset * offset
    return jnp.where(jnp.abs(offset) <= radius, value, 0).astype(F32).astype(BF16)


def split(value):
    high = value.astype(BF16)
    return high, (value - high.astype(F32)).astype(BF16)


def iota(shape, dim):
    return lax.broadcasted_iota(jnp.int32, shape, dim)


def kernel(dens, eff, outv, ext, effv, xb, zb, zm, hold, zsend, zrecv, wy, wm, wh, wl, late, tsend, trecv, up_in, wrap_in, beside_in, peers_in, sent, e_recv, m_recv, l_recv, t_recv,
           y_recv, f_recv, z_recv, own_sem, eff_sem):
    snaps, nx, ny, nz = dens.shape
    rows = ny + 2 * H
    groups = rows // GROUP
    strips = ny // STRIP
    wide = STRIP + 2 * H
    inner = ny - 2 * H
    final = snaps - 1
    units = snaps * strips
    everything = pl.ds(0, snaps)
    near = {}
    for axis in ("gx", "gy", "gz"):
        count = lax.axis_size(axis)
        me = lax.axis_index(axis)
        near[axis] = (lax.rem(me + 1, count), lax.rem(me + count - 1, count))
    up, down = ({"gx": near["gx"][d]} for d in range(2))
    peers = [{axis: near[axis][d]} for axis in ("gy", "gz") for d in range(2)]
    first = lax.axis_index("gx") == 0
    last = lax.axis_index("gx") == lax.axis_size("gx") - 1

    own_copy = pltpu.make_async_copy(
        dens, ext.at[everything, pl.ds(H, nx), pl.ds(H, ny)], own_sem)
    eff_copy = pltpu.make_async_copy(eff, effv, eff_sem)

    def landed(ref, sem):
        pltpu.make_async_copy(ref, ref, sem).wait()

    def edge_copies(d):
        source = nx - H if d == 0 else 0
        target = 0 if d == 0 else nx + H
        return [pltpu.make_async_remote_copy(
            src_ref=dens.at[everything, pl.ds(source, H), pl.ds(start, H)],
            dst_ref=ext.at[everything, pl.ds(target, H), pl.ds(H + start, H)],
            send_sem=sent.at[0], recv_sem=e_recv,
            device_id=up if d == 0 else down, device_id_type=MESH) for start in (0, ny - H)]

    def middle_copy(s, d):
        return pltpu.make_async_remote_copy(
            src_ref=dens.at[s, pl.ds(nx - H if d == 0 else 0, H), pl.ds(H, inner)],
            dst_ref=ext.at[s, pl.ds(0 if d == 0 else nx + H, H), pl.ds(2 * H, inner)],
            send_sem=sent.at[0], recv_sem=m_recv.at[s],
            device_id=up if d == 0 else down, device_id_type=MESH)

    def late_copy(far, d):
        count = LATE if far else H - LATE
        skip = 0 if far == (d == 0) else H - count
        return pltpu.make_async_remote_copy(
            src_ref=dens.at[final, pl.ds((nx - H if d == 0 else 0) + skip, count), pl.ds(H, inner)],
            dst_ref=late.at[d, pl.ds(skip, count)],
            send_sem=sent.at[0], recv_sem=l_recv.at[far],
            device_id=up if d == 0 else down, device_id_type=MESH)

    def t_copy(d):
        return pltpu.make_async_remote_copy(
            src_ref=tsend.at[d], dst_ref=trecv.at[d],
            send_sem=sent.at[1], recv_sem=t_recv,
            device_id=up if d == 0 else down, device_id_type=MESH)

    def y_copy(d):
        source = ny - H if d == 0 else 0
        target = 0 if d == 0 else ny + H
        return pltpu.make_async_remote_copy(
            src_ref=dens.at[everything, pl.ds(0, nx), pl.ds(source, H)],
            dst_ref=ext.at[everything, pl.ds(H, nx), pl.ds(target, H)],
            send_sem=sent.at[2], recv_sem=y_recv,
            device_id={"gy": near["gy"][d]}, device_id_type=MESH)

    def f_copy(q, d):
        planes = 0 if q == 0 else nx + H
        source = ny if d == 0 else H
        target = 0 if d == 0 else ny + H
        return pltpu.make_async_remote_copy(
            src_ref=ext.at[everything, pl.ds(planes, H), pl.ds(source, H)],
            dst_ref=ext.at[everything, pl.ds(planes, H), pl.ds(target, H)],
            send_sem=sent.at[3], recv_sem=f_recv,
            device_id={"gy": near["gy"][d]}, device_id_type=MESH)

    def z_copy(u, d):
        return pltpu.make_async_remote_copy(
            src_ref=zsend.at[u, d], dst_ref=zrecv.at[u, d],
            send_sem=sent.at[4], recv_sem=z_recv.at[u],
            device_id={"gz": near["gz"][d]}, device_id_type=MESH)

    def tell(sem, device):
        pl.semaphore_signal(sem, inc=1, device_id=device, device_id_type=MESH)

    def start(*copies):
        for copy in copies:
            copy.start()

    own_copy.start()
    eff_copy.start()

    barrier = pltpu.get_barrier_semaphore()

    @pl.when(first)
    def _():
        tell(barrier, up)
        for peer in peers:
            tell(barrier, peer)
        pl.semaphore_wait(barrier, len(peers))

    @pl.when(jnp.logical_not(first))
    def _():
        pl.semaphore_wait(barrier, 1)

        @pl.when(jnp.logical_not(last))
        def _():
            tell(barrier, up)
        tell(up_in, down)

        @pl.when(last)
        def _():
            tell(wrap_in, up)
            for pair in zip(edge_copies(0), edge_copies(1)):
                start(*pair)

        @pl.when(jnp.logical_not(last))
        def _():
            start(*edge_copies(1))

    @pl.when(jnp.logical_not(last))
    def _():
        pl.semaphore_wait(up_in, 1)
        start(*edge_copies(0))

    own_copy.wait()
    slot_of = lax.div(iota((inner, nz), 1), 2 * H)
    for d in range(2):
        packed = jnp.zeros((inner, nz), F32)
        for p in range(H):
            block = ext[final, (nx if d == 0 else H) + p, pl.ds(2 * H, inner)]
            rolled = pltpu.roll(block, (p * 2 * H + H) % nz, 1)
            packed = jnp.where(slot_of == p, rolled, packed)
        tsend[d] = packed

    def rest(d):
        return ([t_copy(d)] + [middle_copy(s, d) for s in range(final)]
                + [late_copy(far, d) for far in range(2)])

    def meet_peers():
        for peer in peers:
            tell(beside_in, peer)
        pl.semaphore_wait(beside_in, len(peers))
        tell(peers_in, up)

    @pl.when(first)
    def _():
        meet_peers()
        pl.semaphore_wait(wrap_in, 1)
        start(*edge_copies(1))
        for pair in zip(rest(0), rest(1)):
            start(*pair)

    @pl.when(jnp.logical_not(first))
    def _():
        for pair in zip(rest(0), rest(1)):
            start(*pair)

    for f, radius in enumerate(RADII):
        shape = (STRIP, wide)
        along = band(iota(shape, 1) - iota(shape, 0) - H, radius)
        wy[f] = jnp.concatenate([along, along], axis=1)
        shape = (nz, nz)
        along = band(iota(shape, 1) - iota(shape, 0), radius)
        wm[f] = jnp.concatenate([along, along], axis=0)
        shape = (nx * H, nz)
        slot = lax.div(iota(shape, 0), H)
        cell = lax.rem(iota(shape, 0), H)
        lane = iota(shape, 1)
        low = band(cell - H - lane, radius)
        high = band(cell + nz - lane, radius)
        zero = jnp.zeros_like(low)
        for p in range(nx):
            low_p = jnp.where(slot == p, low, zero)
            high_p = jnp.where(slot == (p + 1) % nx, high, zero)
            wh[f, p // 2, pl.ds(0, nx * H), pl.ds((p % 2) * nz, nz)] = low_p
            wh[f, p // 2, pl.ds(nx * H, nx * H), pl.ds((p % 2) * nz, nz)] = high_p
    shape = (ny, inner)
    for f, radius in enumerate(RADII):
        along = band(iota(shape, 1) + H - iota(shape, 0), radius)
        wl[f] = jnp.concatenate([along, along], axis=1)

    @pl.when(jnp.logical_not(first))
    def _():
        pl.semaphore_wait(peers_in, 1)

        @pl.when(jnp.logical_not(last))
        def _():
            meet_peers()

    for d in range(2):
        y_copy(d).start()
    landed(ext.at[everything, pl.ds(0, 2 * H), pl.ds(0, 2 * H)], e_recv)
    for d in range(2):
        for q in range(2):
            f_copy(q, d).start()

    def smooth_x(field, start, g):
        base = g * GROUP

        def one(i, carry):
            def plane(k):
                return field[i + (H + k), pl.ds(start, GROUP)]

            center = plane(0)
            sums = [center * float((radius + 1) ** 2) for radius in RADII]
            for k in range(1, R_LARGE + 1):
                pair = plane(-k) + plane(k)
                for f, radius in enumerate(RADII):
                    if k <= radius:
                        sums[f] = sums[f] + pair * float((radius + 1) ** 2 - k * k)
            for f in range(2):
                high, low = split(sums[f])
                xb[f, i, pl.ds(base, GROUP)] = high
                xb[f, i, pl.ds(rows + base, GROUP)] = low
            return carry

        lax.fori_loop(0, nx, one, 0, unroll=16)

    lane_slots = lax.div(iota((STRIP, nz), 1), H)

    def smooth_y(u):
        base = (u % strips) * STRIP
        for f in range(2):
            to_up = jnp.zeros((STRIP, nz), F32)
            to_down = jnp.zeros((STRIP, nz), F32)
            for p in range(0, nx, 2):
                both = jnp.concatenate(
                    [jnp.concatenate([xb[f, p + j, pl.ds(base, wide)],
                                      xb[f, p + j, pl.ds(rows + base, wide)]], axis=0)
                     for j in range(2)], axis=1)
                done = jnp.dot(wy[f], both, preferred_element_type=F32)
                for j in range(2):
                    value = done[:, j * nz:(j + 1) * nz]
                    rolled = pltpu.roll(value, ((p + j + 1) * H) % nz, 1)
                    to_up = jnp.where(lane_slots == p + j, rolled, to_up)
                    to_down = jnp.where(lane_slots == (p + j + 1) % nx, rolled, to_down)
                    high, low = split(value)
                    zb[f, p + j, :, pl.ds(0, nz)] = high
                    zb[f, p + j, :, pl.ds(nz, nz)] = low
            zsend[u, 0, pl.ds(f * STRIP, STRIP)] = to_up
            zsend[u, 1, pl.ds(f * STRIP, STRIP)] = to_down
        for d in range(2):
            z_copy(u, d).start()

    def main_z(u):
        s, h = divmod(u, strips)
        for f in range(2):
            for p in range(0, nx, 8):
                block = zb[f, pl.ds(p, 8)].reshape(8 * STRIP, 2 * nz)
                done = jnp.dot(block, wm[f], preferred_element_type=F32).reshape(8, STRIP, nz)
                if s == final:
                    hold[f, pl.ds(p, 8), pl.ds(h * STRIP, STRIP)] = done
                else:
                    zm[h, f, pl.ds(p, 8)] = done

    def ionized(small, large, share):
        levels = [share * (total * scale_of(radius)) - less
                  for total, radius, less in zip((small, large), RADII, (0.3, 0.1))]
        return jnp.clip(0.5 + 0.25 * jnp.maximum(*levels), 0.0, 1.0)

    def finish(u):
        s, h = divmod(u, strips)
        part = pl.ds(h * STRIP, STRIP)
        landed(zrecv.at[u], z_recv.at[u])
        halves = []
        for f in range(2):
            own = pl.ds(f * STRIP, STRIP)
            packed = jnp.concatenate([zrecv[u, 0, own], zrecv[u, 1, own]], axis=1)
            halves.append(jnp.concatenate(split(packed), axis=0))
        for p in range(0, nx, 2):
            halo = []
            for f in range(2):
                done = jnp.dot(halves[f], wh[f, p // 2], preferred_element_type=F32)
                halo.append(done[:STRIP] + done[STRIP:])
            for j in range(2):
                small, large = (done[:, j * nz:(j + 1) * nz] for done in halo)
                if s == final:
                    hold[0, p + j, part] += small
                    hold[1, p + j, part] += large
                else:
                    outv[s, p + j, part] = ionized(
                        zm[h, 0, p + j] + small, zm[h, 1, p + j] + large, effv[p + j, part])

    def unpack():
        landed(trecv, t_recv)
        lane = iota((inner, nz), 1)
        outer = (lane < H) | (lane >= nz - H)
        for d in range(2):
            packed = trecv[d]
            for p in range(H):
                block = pltpu.roll(packed, (2 * nz - p * 2 * H - H) % nz, 1)
                ext[final, (0 if d == 0 else nx + H) + p, pl.ds(2 * H, inner)] = jnp.where(
                    outer, block, 0.0)

    def add_late(far):
        count = LATE if far else H - LATE
        landed(late.at[pl.ds(0, 2), pl.ds(0, count)], l_recv.at[far])
        lane = iota((inner, nz), 1)
        inside = (lane >= H) & (lane < nz - H)
        distances = range(H - LATE + 1, H + 1) if far else range(1, H - LATE + 1)
        planes = [{k: jnp.where(inside, late[d, H - k if d == 0 else k - 1], 0.0) for k in distances}
                  for d in range(2)]
        for f, radius in enumerate(RADII):
            moved = []
            for d in range(2):
                for i in range(radius + 1 - distances[0]):
                    total = None
                    for k in distances:
                        if k + i <= radius:
                            term = planes[d][k] * float((radius + 1) ** 2 - (k + i) ** 2)
                            total = term if total is None else total + term
                    moved.append((i if d == 0 else nx - 1 - i, total))
            for n in range(0, len(moved), 4):
                some = moved[n:n + 4]
                blocks = []
                for m in range(0, len(some), 2):
                    both = jnp.concatenate(
                        [jnp.concatenate(split(total), axis=0) for _, total in some[m:m + 2]], axis=1)
                    done = jnp.dot(wl[f], both, preferred_element_type=F32)
                    for j in range(len(some[m:m + 2])):
                        blocks.append(jnp.concatenate(split(done[:, j * nz:(j + 1) * nz]), axis=1))
                done = jnp.dot(jnp.concatenate(blocks, axis=0), wm[f], preferred_element_type=F32)
                for j, (p, _) in enumerate(some):
                    add = done[j * ny:(j + 1) * ny]
                    if far:
                        outv[final, p] = ionized(hold[0, p], hold[1, p] + add, effv[p])
                    else:
                        hold[f, p] += add
        if not far:
            for p in range(LATE, nx - LATE):
                outv[final, p] = ionized(hold[0, p], hold[1, p], effv[p])

    landed(ext.at[everything, pl.ds(0, nx), pl.ds(0, 2 * H)], y_recv)
    landed(ext.at[everything, pl.ds(0, 2 * H), pl.ds(0, 2 * H)], f_recv)
    eff_copy.wait()
    unpack()

    def smooth(s):
        if s != final:
            landed(ext.at[s, pl.ds(0, 2 * H), pl.ds(0, inner)], m_recv.at[s])
        for g in range(groups):
            smooth_x(ext.at[s], g * GROUP, g)
        for u in range(s * strips, (s + 1) * strips):
            smooth_y(u)
            main_z(u)

    def complete(s):
        for u in range(s * strips, (s + 1) * strips):
            finish(u)

    smooth(final)
    for s in range(final):
        smooth(s)
        if s == 0:
            complete(final)
        complete(s)
    for far in range(2):
        add_late(far)

    landed(ext.at[everything, pl.ds(0, 2 * H), pl.ds(0, ny)], sent.at[0])
    landed(tsend, sent.at[1])
    landed(ext.at[everything, pl.ds(0, nx), pl.ds(0, 2 * H)], sent.at[2])
    landed(ext.at[everything, pl.ds(0, 2 * H), pl.ds(0, 2 * H)], sent.at[3])
    landed(zsend, sent.at[4])


def on_device(density, efficiency):
    snaps, nx, ny, nz = density.shape
    rows = ny + 2 * H
    inner = ny - 2 * H
    units = snaps * (ny // STRIP)
    dma = pltpu.SemaphoreType.DMA
    told = pltpu.SemaphoreType.REGULAR
    return pl.pallas_call(
        kernel,
        out_shape=pltpu.VMEM(density.shape, F32),
        in_specs=[pl.BlockSpec(memory_space=pl.ANY)] * 2,
        out_specs=pl.BlockSpec(memory_space=pltpu.VMEM),
        scratch_shapes=[
            pltpu.VMEM((snaps, nx + 2 * H, rows, nz), F32),
            pltpu.VMEM((nx, ny, nz), F32),
            pltpu.VMEM((2, nx, 2 * rows, nz), BF16),
            pltpu.VMEM((2, nx, STRIP, 2 * nz), BF16),
            pltpu.VMEM((ny // STRIP, 2, nx, STRIP, nz), F32),
            pltpu.VMEM((2, nx, ny, nz), F32),
            pltpu.VMEM((units, 2, 2 * STRIP, nx * H), F32),
            pltpu.VMEM((units, 2, 2 * STRIP, nx * H), F32),
            pltpu.VMEM((2, STRIP, 2 * (STRIP + 2 * H)), BF16),
            pltpu.VMEM((2, 2 * nz, nz), BF16),
            pltpu.VMEM((2, nx // 2, 2 * nx * H, 2 * nz), BF16),
            pltpu.VMEM((2, ny, 2 * inner), BF16),
            pltpu.VMEM((2, H, inner, nz), F32),
            pltpu.VMEM((2, inner, nz), F32),
            pltpu.VMEM((2, inner, nz), F32),
            told, told, told, told,
            dma((5,)), dma, dma((snaps - 1,)), dma((2,)), dma, dma, dma, dma((units,)), dma, dma,
        ],
        compiler_params=pltpu.CompilerParams(
            collective_id=0, has_side_effects=True),
    )(density, efficiency)


def solution(mesh):
    placed = (P(None, "gx", "gy", "gz"), P("gx", "gy", "gz"))
    return jax.shard_map(
        on_device, mesh=mesh, in_specs=placed, out_specs=P(None, "gx", "gy", "gz"), check_vma=False
    )
```

```python
import math

import jax
import jax.numpy as jnp
from jax import lax
from jax.experimental import pallas as pl
from jax.experimental.pallas import tpu as pltpu
from jax.sharding import PartitionSpec as P

R_SMALL = 4
R_LARGE = 8
RADII = (R_SMALL, R_LARGE)
H = R_LARGE
GROUP = 16
STRIP = 32
LATE = 4
F32 = jnp.float32
BF16 = jnp.bfloat16
MESH = pl.DeviceIdType.MESH


def scale_of(radius):
    raw = [(radius + 1) ** 2 - k * k for k in range(-radius, radius + 1)]
    return 1.0 / math.sqrt(sum(value * value for value in raw)) ** 3


def band(offset, radius):
    value = (radius + 1) ** 2 - offset * offset
    return jnp.where(jnp.abs(offset) <= radius, value, 0).astype(F32).astype(BF16)


def split(value):
    high = value.astype(BF16)
    return high, (value - high.astype(F32)).astype(BF16)


def iota(shape, dim):
    return lax.broadcasted_iota(jnp.int32, shape, dim)


def kernel(dens, eff, outv, ext, effv, xb, zb, hold, zsend, zrecv, wy, wm, wh, wl, msend, mrecv, tsend, trecv, up_in, wrap_in, beside_in, peers_in, sent, e_recv, m_recv, t_recv,
           y_recv, f_recv, z_recv, own_sem, eff_sem):
    snaps, nx, ny, nz = dens.shape
    rows = ny + 2 * H
    groups = rows // GROUP
    strips = ny // STRIP
    wide = STRIP + 2 * H
    inner = ny - 2 * H
    final = snaps - 1
    units = snaps * strips
    everything = pl.ds(0, snaps)
    near = {}
    for axis in ("gx", "gy", "gz"):
        count = lax.axis_size(axis)
        me = lax.axis_index(axis)
        near[axis] = (lax.rem(me + 1, count), lax.rem(me + count - 1, count))
    up, down = ({"gx": near["gx"][d]} for d in range(2))
    peers = [{axis: near[axis][d]} for axis in ("gy", "gz") for d in range(2)]
    first = lax.axis_index("gx") == 0
    last = lax.axis_index("gx") == lax.axis_size("gx") - 1

    own_copy = pltpu.make_async_copy(
        dens, ext.at[everything, pl.ds(H, nx), pl.ds(H, ny)], own_sem)
    eff_copy = pltpu.make_async_copy(eff, effv, eff_sem)

    def landed(ref, sem):
        pltpu.make_async_copy(ref, ref, sem).wait()

    def edge_copies(d):
        source = nx - H if d == 0 else 0
        target = 0 if d == 0 else nx + H
        return [pltpu.make_async_remote_copy(
            src_ref=dens.at[everything, pl.ds(source, H), pl.ds(start, H)],
            dst_ref=ext.at[everything, pl.ds(target, H), pl.ds(H + start, H)],
            send_sem=sent.at[0], recv_sem=e_recv,
            device_id=up if d == 0 else down, device_id_type=MESH) for start in (0, ny - H)]

    def middle_copies(s, d):
        cuts = ((0, H - LATE), (H - LATE, LATE - 1)) if s == final else ((0, H - 1),)
        return [pltpu.make_async_remote_copy(
            src_ref=msend.at[s, d, pl.ds(start, count)], dst_ref=mrecv.at[s, d, pl.ds(start, count)],
            send_sem=sent.at[5], recv_sem=m_recv.at[s + far],
            device_id=up if d == 0 else down, device_id_type=MESH)
            for far, (start, count) in enumerate(cuts)]

    def t_copy(d):
        return pltpu.make_async_remote_copy(
            src_ref=tsend.at[d], dst_ref=trecv.at[d],
            send_sem=sent.at[1], recv_sem=t_recv,
            device_id=up if d == 0 else down, device_id_type=MESH)

    def y_copy(d):
        source = ny - H if d == 0 else 0
        target = 0 if d == 0 else ny + H
        return pltpu.make_async_remote_copy(
            src_ref=dens.at[everything, pl.ds(0, nx), pl.ds(source, H)],
            dst_ref=ext.at[everything, pl.ds(H, nx), pl.ds(target, H)],
            send_sem=sent.at[2], recv_sem=y_recv,
            device_id={"gy": near["gy"][d]}, device_id_type=MESH)

    def f_copy(q, d):
        planes = 0 if q == 0 else nx + H
        source = ny if d == 0 else H
        target = 0 if d == 0 else ny + H
        return pltpu.make_async_remote_copy(
            src_ref=ext.at[everything, pl.ds(planes, H), pl.ds(source, H)],
            dst_ref=ext.at[everything, pl.ds(planes, H), pl.ds(target, H)],
            send_sem=sent.at[3], recv_sem=f_recv,
            device_id={"gy": near["gy"][d]}, device_id_type=MESH)

    def z_copy(u, d):
        return pltpu.make_async_remote_copy(
            src_ref=zsend.at[u, d], dst_ref=zrecv.at[u, d],
            send_sem=sent.at[4], recv_sem=z_recv.at[u],
            device_id={"gz": near["gz"][d]}, device_id_type=MESH)

    def tell(sem, device):
        pl.semaphore_signal(sem, inc=1, device_id=device, device_id_type=MESH)

    def start(*copies):
        for copy in copies:
            copy.start()

    own_copy.start()
    eff_copy.start()

    barrier = pltpu.get_barrier_semaphore()

    @pl.when(first)
    def _():
        tell(barrier, up)
        for peer in peers:
            tell(barrier, peer)
        pl.semaphore_wait(barrier, len(peers))

    @pl.when(jnp.logical_not(first))
    def _():
        pl.semaphore_wait(barrier, 1)

        @pl.when(jnp.logical_not(last))
        def _():
            tell(barrier, up)
        tell(up_in, down)

        @pl.when(last)
        def _():
            tell(wrap_in, up)
            start(*edge_copies(0), *edge_copies(1))

        @pl.when(jnp.logical_not(last))
        def _():
            start(*edge_copies(1))

    @pl.when(jnp.logical_not(last))
    def _():
        pl.semaphore_wait(up_in, 1)
        start(*edge_copies(0))

    own_copy.wait()
    lane = iota((inner, nz), 1)
    outer = (lane < H) | (lane >= nz - H)
    outer_slot = lax.div(lane, 2 * H)
    inner_slot = lax.div(lane + H, 2 * H)
    inner_rows = pl.ds(2 * H, inner)
    for s in range(snaps):
        for d in range(2):
            planes = [ext[s, H + (nx - k if d == 0 else k - 1), inner_rows] for k in range(1, H + 1)]
            packed = jnp.zeros((inner, nz), F32)
            for j, plane in enumerate(planes):
                packed = jnp.where(outer_slot == j, pltpu.roll(plane, (j * 2 * H + H) % nz, 1), packed)
            tsend[d, s] = packed
            for j, plane in enumerate(planes[:-1]):
                moved = pltpu.roll(planes[-1], (nz - (j + 1) * 2 * H) % nz, 1)
                msend[s, d, j] = jnp.where(outer, moved, plane)

    def start_rest(order):
        for kind, d in order:
            if kind == "T":
                t_copy(d).start()
            else:
                start(*middle_copies(kind, d))

    def meet_peers():
        for peer in peers:
            tell(beside_in, peer)
        pl.semaphore_wait(beside_in, len(peers))
        tell(peers_in, up)

    @pl.when(first)
    def _():
        meet_peers()
        pl.semaphore_wait(wrap_in, 1)
        start(*edge_copies(1))
        start_rest([("T", 0), ("T", 1), (0, 0), (0, 1), (1, 0), (1, 1), (2, 0), (2, 1)])

    @pl.when(jnp.logical_not(first))
    def _():
        start_rest([("T", 1), ("T", 0), (0, 0), (0, 1), (1, 0), (1, 1), (2, 0), (2, 1)])

    for f, radius in enumerate(RADII):
        shape = (STRIP, wide)
        along = band(iota(shape, 1) - iota(shape, 0) - H, radius)
        wy[f] = jnp.concatenate([along, along], axis=1)
        shape = (nz, nz)
        along = band(iota(shape, 1) - iota(shape, 0), radius)
        wm[f] = jnp.concatenate([along, along], axis=0)
        shape = (nx * H, nz)
        slot = lax.div(iota(shape, 0), H)
        cell = lax.rem(iota(shape, 0), H)
        lane = iota(shape, 1)
        low = band(cell - H - lane, radius)
        high = band(cell + nz - lane, radius)
        zero = jnp.zeros_like(low)
        for p in range(nx):
            low_p = jnp.where(slot == p, low, zero)
            high_p = jnp.where(slot == (p + 1) % nx, high, zero)
            wh[f, p // 2, pl.ds(0, nx * H), pl.ds((p % 2) * nz, nz)] = low_p
            wh[f, p // 2, pl.ds(nx * H, nx * H), pl.ds((p % 2) * nz, nz)] = high_p
    shape = (ny, inner)
    for f, radius in enumerate(RADII):
        along = band(iota(shape, 1) + H - iota(shape, 0), radius)
        wl[f] = jnp.concatenate([along, along], axis=1)

    @pl.when(jnp.logical_not(first))
    def _():
        pl.semaphore_wait(peers_in, 1)

        @pl.when(jnp.logical_not(last))
        def _():
            meet_peers()

    for d in range(2):
        y_copy(d).start()
    landed(ext.at[everything, pl.ds(0, 2 * H), pl.ds(0, 2 * H)], e_recv)
    for d in range(2):
        for q in range(2):
            f_copy(q, d).start()

    def smooth_x(field, start, g):
        base = g * GROUP

        def one(i, carry):
            def plane(k):
                return field[i + (H + k), pl.ds(start, GROUP)]

            center = plane(0)
            sums = [center * float((radius + 1) ** 2) for radius in RADII]
            for k in range(1, R_LARGE + 1):
                pair = plane(-k) + plane(k)
                for f, radius in enumerate(RADII):
                    if k <= radius:
                        sums[f] = sums[f] + pair * float((radius + 1) ** 2 - k * k)
            for f in range(2):
                high, low = split(sums[f])
                xb[f, i, pl.ds(base, GROUP)] = high
                xb[f, i, pl.ds(rows + base, GROUP)] = low
            return carry

        lax.fori_loop(0, nx, one, 0, unroll=16)

    lane_slots = lax.div(iota((STRIP, nz), 1), H)

    def smooth_y(u):
        base = (u % strips) * STRIP
        for f in range(2):
            to_up = jnp.zeros((STRIP, nz), F32)
            to_down = jnp.zeros((STRIP, nz), F32)
            for p in range(0, nx, 2):
                both = jnp.concatenate(
                    [jnp.concatenate([xb[f, p + j, pl.ds(base, wide)],
                                      xb[f, p + j, pl.ds(rows + base, wide)]], axis=0)
                     for j in range(2)], axis=1)
                done = jnp.dot(wy[f], both, preferred_element_type=F32)
                for j in range(2):
                    value = done[:, j * nz:(j + 1) * nz]
                    rolled = pltpu.roll(value, ((p + j + 1) * H) % nz, 1)
                    to_up = jnp.where(lane_slots == p + j, rolled, to_up)
                    to_down = jnp.where(lane_slots == (p + j + 1) % nx, rolled, to_down)
                    high, low = split(value)
                    zb[f, p + j, :, pl.ds(0, nz)] = high
                    zb[f, p + j, :, pl.ds(nz, nz)] = low
            zsend[u, 0, pl.ds(f * STRIP, STRIP)] = to_up
            zsend[u, 1, pl.ds(f * STRIP, STRIP)] = to_down
        for d in range(2):
            z_copy(u, d).start()

    def main_z(u):
        s, h = divmod(u, strips)
        for f in range(2):
            for p in range(0, nx, 8):
                block = zb[f, pl.ds(p, 8)].reshape(8 * STRIP, 2 * nz)
                done = jnp.dot(block, wm[f], preferred_element_type=F32).reshape(8, STRIP, nz)
                hold[s, f, pl.ds(p, 8), pl.ds(h * STRIP, STRIP)] = done

    def ionized(small, large, share):
        levels = [share * (total * scale_of(radius)) - less
                  for total, radius, less in zip((small, large), RADII, (0.3, 0.1))]
        return jnp.clip(0.5 + 0.25 * jnp.maximum(*levels), 0.0, 1.0)

    def finish(u):
        s, h = divmod(u, strips)
        part = pl.ds(h * STRIP, STRIP)
        landed(zrecv.at[u], z_recv.at[u])
        halves = []
        for f in range(2):
            own = pl.ds(f * STRIP, STRIP)
            packed = jnp.concatenate([zrecv[u, 0, own], zrecv[u, 1, own]], axis=1)
            halves.append(jnp.concatenate(split(packed), axis=0))
        for p in range(0, nx, 2):
            halo = []
            for f in range(2):
                done = jnp.dot(halves[f], wh[f, p // 2], preferred_element_type=F32)
                halo.append(done[:STRIP] + done[STRIP:])
            for j in range(2):
                for f in range(2):
                    hold[s, f, p + j, part] += halo[f][:, j * nz:(j + 1) * nz]

    def unpack():
        landed(trecv, t_recv)
        for s in range(snaps):
            for d in range(2):
                for j in range(H):
                    block = pltpu.roll(trecv[d, s], (2 * nz - j * 2 * H - H) % nz, 1)
                    ext[s, H - 1 - j if d == 0 else nx + H + j, inner_rows] = jnp.where(outer, block, 0.0)

    def add_late(s, part):
        far = s == final and part == 1
        near = s == final and part == 0
        low, high = (1, H - LATE) if near else (H - LATE + 1, H) if far else (1, H)
        begin, end = low - 1, min(high, H - 1)
        landed(mrecv.at[s, pl.ds(0, 2), pl.ds(begin, end - begin)], m_recv.at[s + part])
        planes = [{}, {}]
        for d in range(2):
            for k in range(low, end + 1):
                planes[d][k] = jnp.where(outer, 0.0, mrecv[s, d, k - 1])
            if not near:
                spread = jnp.zeros((inner, nz), F32)
                for j in range(H - 1):
                    block = pltpu.roll(mrecv[s, d, j], (j + 1) * 2 * H % nz, 1)
                    spread = jnp.where(inner_slot == j + 1, block, spread)
                planes[d][H] = jnp.where(outer, 0.0, spread)
        for f, radius in enumerate(RADII):
            moved = []
            for d in range(2):
                for i in range(radius + 1 - low):
                    total = None
                    for k in range(low, high + 1):
                        if k + i <= radius:
                            term = planes[d][k] * float((radius + 1) ** 2 - (k + i) ** 2)
                            total = term if total is None else total + term
                    moved.append((i if d == 0 else nx - 1 - i, total))
            for n in range(0, len(moved), 4):
                some = moved[n:n + 4]
                blocks = []
                for m in range(0, len(some), 2):
                    both = jnp.concatenate(
                        [jnp.concatenate(split(total), axis=0) for _, total in some[m:m + 2]], axis=1)
                    done = jnp.dot(wl[f], both, preferred_element_type=F32)
                    for j in range(len(some[m:m + 2])):
                        blocks.append(jnp.concatenate(split(done[:, j * nz:(j + 1) * nz]), axis=1))
                done = jnp.dot(jnp.concatenate(blocks, axis=0), wm[f], preferred_element_type=F32)
                for j, (p, _) in enumerate(some):
                    total = hold[s, f, p] + done[j * ny:(j + 1) * ny]
                    if f == 0 or (near and not LATE <= p < nx - LATE):
                        hold[s, f, p] = total
                    else:
                        outv[s, p] = ionized(hold[s, 0, p], total, effv[p])

    landed(ext.at[everything, pl.ds(0, nx), pl.ds(0, 2 * H)], y_recv)
    landed(ext.at[everything, pl.ds(0, 2 * H), pl.ds(0, 2 * H)], f_recv)
    eff_copy.wait()
    unpack()
    for s in range(snaps):
        for g in range(groups):
            smooth_x(ext.at[s], g * GROUP, g)
        for u in range(s * strips, (s + 1) * strips):
            smooth_y(u)
            main_z(u)
    for s in range(snaps):
        for u in range(s * strips, (s + 1) * strips):
            finish(u)
        for part in range(2 if s == final else 1):
            add_late(s, part)

    landed(ext.at[everything, pl.ds(0, 2 * H), pl.ds(0, 2 * H)], sent.at[0])
    landed(msend, sent.at[5])
    landed(tsend, sent.at[1])
    landed(ext.at[everything, pl.ds(0, nx), pl.ds(0, 2 * H)], sent.at[2])
    landed(ext.at[everything, pl.ds(0, 2 * H), pl.ds(0, 2 * H)], sent.at[3])
    landed(zsend, sent.at[4])


def on_device(density, efficiency):
    snaps, nx, ny, nz = density.shape
    rows = ny + 2 * H
    inner = ny - 2 * H
    units = snaps * (ny // STRIP)
    dma = pltpu.SemaphoreType.DMA
    told = pltpu.SemaphoreType.REGULAR
    return pl.pallas_call(
        kernel,
        out_shape=pltpu.VMEM(density.shape, F32),
        in_specs=[pl.BlockSpec(memory_space=pl.ANY)] * 2,
        out_specs=pl.BlockSpec(memory_space=pltpu.VMEM),
        scratch_shapes=[
            pltpu.VMEM((snaps, nx + 2 * H, rows, nz), F32),
            pltpu.VMEM((nx, ny, nz), F32),
            pltpu.VMEM((2, nx, 2 * rows, nz), BF16),
            pltpu.VMEM((2, nx, STRIP, 2 * nz), BF16),
            pltpu.VMEM((snaps, 2, nx, ny, nz), F32),
            pltpu.VMEM((units, 2, 2 * STRIP, nx * H), F32),
            pltpu.VMEM((units, 2, 2 * STRIP, nx * H), F32),
            pltpu.VMEM((2, STRIP, 2 * (STRIP + 2 * H)), BF16),
            pltpu.VMEM((2, 2 * nz, nz), BF16),
            pltpu.VMEM((2, nx // 2, 2 * nx * H, 2 * nz), BF16),
            pltpu.VMEM((2, ny, 2 * inner), BF16),
            pltpu.VMEM((snaps, 2, H - 1, inner, nz), F32),
            pltpu.VMEM((snaps, 2, H - 1, inner, nz), F32),
            pltpu.VMEM((2, snaps, inner, nz), F32),
            pltpu.VMEM((2, snaps, inner, nz), F32),
            told, told, told, told,
            dma((6,)), dma, dma((snaps + 1,)), dma, dma, dma, dma((units,)), dma, dma,
        ],
        compiler_params=pltpu.CompilerParams(
            collective_id=0, has_side_effects=True),
    )(density, efficiency)


def solution(mesh):
    placed = (P(None, "gx", "gy", "gz"), P("gx", "gy", "gz"))
    return jax.shard_map(
        on_device, mesh=mesh, in_specs=placed, out_specs=P(None, "gx", "gy", "gz"), check_vma=False
    )
```
